32 devices in a mesh: elem: 8 (over z, x), span: 4 (over y, core).
Axes of the slice: x: 2, y: 2, z: 4, core: 2. Of those that a mesh axis runs over, the one named last changes fastest.
Arguments:
- column_state: bfloat16 [24576, 1152], P(('elem', 'span')), may hold values from -6 to 6
- counts: int32 [32], replicated, may hold values from 128 to 768, as said below
- edge_index: int32 [32, 4, 16], P(('elem', 'span')), may hold values from 0 to 127, as said below
- encode_first: bfloat16 [3, 32, 16], replicated, may hold values from -0.875 to 0.875
- encode_second: bfloat16 [8, 3, 32, 32], replicated, may hold values from -0.625 to 0.625
- middle_first: bfloat16 [3, 64, 32], replicated, may hold values from -0.625 to 0.625
- middle_second: bfloat16 [8, 3, 64, 64], replicated, may hold values from -0.4375 to 0.4375
- decode_first: bfloat16 [3, 32, 96], replicated, may hold values from -0.375 to 0.375
- decode_second: bfloat16 [8, 3, 32, 32], replicated, may hold values from -0.625 to 0.625
- output_weight: bfloat16 [3, 16, 32], replicated, may hold values from -0.625 to 0.625
Outputs:
- tendencies: bfloat16 [24576, 1152], P(('elem', 'span'))
The draws below stay inside these ranges and needn't reach their ends.
Inputs may be any that keep to these rules, and one draw needn't show every extreme that they name: counts sum to 8192. `edge_index`: the 64 entries of one owner are distinct.
All inputs are finite; a program needn't handle non-finite values.
Results may differ from the reference program's by a relative error of at most 0.0085.
Values may be sent and summed in bfloat16 or wider, within the bound.
A program may use at most 64 MiB of HBM per device.

```python
import jax
import jax.numpy as jnp
from jax import lax

LEV = 72
F_IN = 16
F_OUT = 16
C1 = 32
C2 = 64
DEPTH = 8
SPAN = 256
COL_MAX = 768
EDGE_N = 16
COLUMNS = 24576
N_ELEM = 8
N_SPAN = 4
DEVICES = 32


def draw_counts(key, part):
    floor_count = SPAN // 2
    top_count = 3 * SPAN
    spread_count = top_count - floor_count
    last = DEVICES - 1
    positions = jnp.arange(DEVICES, dtype=jnp.int32)
    squared = positions * positions // last
    profile = 9 * spread_count // 10 * squared * squared // (last * last)
    profile = jnp.where(positions == last, spread_count, profile).astype(jnp.int32)
    remainder = DEVICES * (SPAN - floor_count) - jnp.sum(profile)
    base_add = remainder // last
    extra_add = remainder % last
    profile = profile + jnp.where(positions < last, base_add + (positions < extra_add).astype(jnp.int32), 0)
    counts_all = (floor_count + profile).astype(jnp.int32)
    return jax.random.permutation(key, counts_all)


def draw_edge_index(key, part):
    keys_all = jax.random.split(jax.random.fold_in(key, 7), DEVICES)

    def one_owner(owner_key):
        chosen = jax.random.permutation(owner_key, SPAN // 2)[:4 * EDGE_N]
        return chosen.reshape(4, EDGE_N).astype(jnp.int32)
    return jax.vmap(one_owner)(keys_all)


def block_levels(rng, extent, shards, low, high):
    loudness = 1.0
    for axis_at, blocks in shards:
        heights = jax.random.uniform(jax.random.fold_in(jax.random.fold_in(rng, 6), axis_at), (blocks,), jnp.float32, low / len(shards), high / len(shards))
        loudness = loudness * jnp.repeat(jnp.exp(heights), extent[axis_at] // blocks).reshape((-1,) + (1,) * (len(extent) - 1 - axis_at))
    return loudness


def centred(rng, shape, scale, bound, pieces=(), kind=jnp.bfloat16):
    factor_of = block_levels(rng, shape, pieces, -0.22, 0.18) if pieces else 1.0
    drawn = jax.random.normal(rng, shape, jnp.float32) * scale * factor_of
    return jnp.minimum(jnp.maximum(drawn, -bound), bound).astype(kind)


def setup_inputs(seed: int = 0) -> dict:
    key_of = jax.random.split(jax.random.key(seed), 11)
    column_state = centred(key_of[0], (COLUMNS, F_IN * LEV), 1.0, 6.0, ((0, 32),))
    counts = draw_counts(jax.random.fold_in(key_of[10], 71), 0)
    edge_index = draw_edge_index(jax.random.fold_in(key_of[10], 71), 0)
    encode_first = centred(key_of[3], (3, C1, F_IN), (3 * F_IN) ** -0.5, 0.875)
    encode_second = centred(key_of[4], (DEPTH, 3, C1, C1), (3 * C1) ** -0.5, 0.625)
    middle_first = centred(key_of[5], (3, C2, C1), (3 * C1) ** -0.5, 0.625)
    middle_second = centred(key_of[6], (DEPTH, 3, C2, C2), (3 * C2) ** -0.5, 0.4375)
    decode_first = centred(key_of[7], (3, C1, C2 + C1), (3 * (C2 + C1)) ** -0.5, 0.375)
    decode_second = centred(key_of[8], (DEPTH, 3, C1, C1), (3 * C1) ** -0.5, 0.625)
    output_weight = centred(key_of[9], (3, F_OUT, C1), (3 * C1) ** -0.5, 0.625)
    return {"column_state": column_state, "counts": counts, "edge_index": edge_index, "encode_first": encode_first, "encode_second": encode_second, "middle_first": middle_first, "middle_second": middle_second, "decode_first": decode_first, "decode_second": decode_second, "output_weight": output_weight}


def conv_levels(profile, weight):
    levels = profile.shape[1]
    padded = jnp.pad(profile, ((0, 0), (1, 1), (0, 0)))
    summed = jnp.zeros((weight.shape[1], levels, profile.shape[2]), jnp.float32)
    for tap_index in range(3):
        summed = summed + jnp.einsum('oi,iln->oln', weight[tap_index].astype(jnp.float32), padded[:, tap_index:tap_index + levels, :].astype(jnp.float32))
    return summed


def residual_stack(hidden, stacked_weights):
    for layer_index in range(DEPTH):
        update = jax.nn.silu(conv_levels(hidden, stacked_weights[layer_index]))
        hidden = (hidden.astype(jnp.float32) + update).astype(jnp.bfloat16)
    return hidden


def network(columns, weights):
    encode_first, encode_second, middle_first, middle_second, decode_first, decode_second, output_weight = weights
    inputs = columns.reshape(columns.shape[0], F_IN, LEV).transpose(1, 2, 0)
    hidden = jax.nn.silu(conv_levels(inputs, encode_first)).astype(jnp.bfloat16)
    skipped = residual_stack(hidden, encode_second)
    pooled = (0.5 * (skipped[:, 0::2].astype(jnp.float32) + skipped[:, 1::2].astype(jnp.float32))).astype(jnp.bfloat16)
    middle = jax.nn.silu(conv_levels(pooled, middle_first)).astype(jnp.bfloat16)
    middle = residual_stack(middle, middle_second)
    raised = jnp.repeat(middle, 2, axis=1)
    joined = jnp.concatenate([raised, skipped], axis=0)
    decoded = jax.nn.silu(conv_levels(joined, decode_first)).astype(jnp.bfloat16)
    decoded = residual_stack(decoded, decode_second)
    result = conv_levels(decoded, output_weight).astype(jnp.bfloat16)
    return result.transpose(2, 0, 1).reshape(columns.shape[0], F_OUT * LEV)


def reference(column_state, counts, edge_index, encode_first, encode_second, middle_first, middle_second, decode_first, decode_second, output_weight):
    weights = (encode_first, encode_second, middle_first, middle_second, decode_first, decode_second, output_weight)
    offsets = jnp.concatenate([jnp.zeros((1,), jnp.int32), jnp.cumsum(counts).astype(jnp.int32)])
    live_ranks = jnp.arange(DEVICES * SPAN, dtype=jnp.int32)
    owner_device = jnp.sum((offsets[None, 1:] <= live_ranks[:, None]).astype(jnp.int32), axis=1).astype(jnp.int32)
    live_rows = (owner_device * COL_MAX + live_ranks - offsets[owner_device]).astype(jnp.int32)

    def run_block(block_rows):
        return network(column_state[block_rows], weights)

    computed = lax.map(run_block, live_rows.reshape(-1, 128)).reshape(DEVICES * SPAN, F_OUT * LEV)
    tendency_all = jnp.zeros((COLUMNS, F_OUT * LEV), jnp.bfloat16).at[live_rows].set(computed)
    by_owner = tendency_all.reshape(DEVICES, COL_MAX, F_OUT * LEV)
    edge_values = jax.vmap(lambda table_rows, index_rows: table_rows[index_rows])(by_owner, edge_index)
    edge_values = edge_values.astype(jnp.float32).reshape(N_ELEM, N_SPAN, 4, EDGE_N, F_OUT * LEV)
    west_edge = 0.5 * (edge_values[:, :, 0] + jnp.roll(edge_values[:, :, 1], 1, axis=0))
    east_edge = 0.5 * (edge_values[:, :, 1] + jnp.roll(edge_values[:, :, 0], -1, axis=0))
    south_edge = 0.5 * (edge_values[:, :, 2] + jnp.roll(edge_values[:, :, 3], 1, axis=1))
    north_edge = 0.5 * (edge_values[:, :, 3] + jnp.roll(edge_values[:, :, 2], -1, axis=1))
    averaged = jnp.stack([west_edge, east_edge, south_edge, north_edge], axis=2).astype(jnp.bfloat16)
    averaged = averaged.reshape(DEVICES, 4, EDGE_N, F_OUT * LEV)
    by_owner = jax.vmap(lambda table_rows, index_rows, values_new: table_rows.at[index_rows.reshape(-1)].set(values_new.reshape(-1, F_OUT * LEV)))(by_owner, edge_index, averaged)
    return by_owner.reshape(COLUMNS, F_OUT * LEV)
```

```python
import functools

import jax
import jax.numpy as jnp
from jax import lax
from jax.experimental import pallas as pl
from jax.experimental.pallas import tpu as pltpu
from jax.sharding import PartitionSpec as P

LEV = 72
HALF = LEV // 2
F_IN = 16
F_OUT = 16
C1 = 32
C2 = 64
DEPTH = 8
FEAT = F_IN * LEV
LANES = 128
NB = 256


def band(weight, levels):
    taps, out, inn = weight.shape[-3:]
    lead = weight.shape[:-3]
    flat = jnp.swapaxes(weight, -3, -2).reshape(lead + (out, taps * inn))
    none = [(0, 0)] * (len(lead) + 1)
    rows = [
        jnp.pad(flat, none + [(inn * d, inn * (levels - 1 - d))]) for d in range(levels)
    ]
    return jnp.concatenate(rows, axis=-2)


def raised_band(weight):
    w = weight.astype(jnp.float32)
    zero = jnp.zeros_like(w[0])
    first, both, late, last = w[0], w[1] + w[2], w[0] + w[1], w[2]
    rows = [
        [first, both, zero, zero],
        [zero, late, last, zero],
        [zero, first, both, zero],
        [zero, zero, late, last],
    ]
    return jnp.concatenate([jnp.concatenate(r, axis=1) for r in rows], axis=0).astype(weight.dtype)


def half_silu(acc):
    return acc + acc * jnp.tanh(acc)


def dot(a, b):
    return jnp.dot(a, b, preferred_element_type=jnp.float32)


def stack_layers(src, dst, w_ref, channels, per, blocks, width):
    def one(layer, source, target):
        w = w_ref[layer]
        for j in range(blocks):
            lo = j * per * channels
            acc = dot(w, source[lo : lo + width, :])
            mid = slice(lo + channels, lo + channels + per * channels)
            target[mid, :] = (source[mid, :].astype(jnp.float32) + half_silu(acc)).astype(jnp.bfloat16)

    def pair(step, carry):
        one(2 * step, src, dst)
        one(2 * step + 1, dst, src)
        return carry

    lax.fori_loop(0, DEPTH // 2, pair, 0)


def net_kernel(
    sizes, x_ref, we1, we2, wm1, wm2, wdm, wds, wd2, wo, y_ref, wide, xin, ha, hb, hc, pool, ma, mb
):
    step = pl.program_id(0)
    live = sizes[0] - step * NB

    @pl.when(step == 0)
    def _():
        xin[...] = jnp.zeros_like(xin)
        for ref in (ha, hb, hc, pool, ma, mb):
            ref[...] = jnp.zeros_like(ref)

    @pl.when(live <= 0)
    def _():
        y_ref[...] = jnp.zeros_like(y_ref)

    @pl.when(live > 0)
    def _():
        for part in range(NB // LANES):
            here = slice(part * LANES, (part + 1) * LANES)
            wide[part] = x_ref[here, :].astype(jnp.float32).T
            for l in range(LEV):
                xin[F_IN * (l + 1) : F_IN * (l + 2), here] = wide[
                    part, pl.ds(l, F_IN, stride=LEV), :
                ].astype(jnp.bfloat16)
        w = we1[...]
        for j in range(12):
            acc = dot(w, xin[96 * j : 96 * j + 128, :])
            ha[192 * j + 32 : 192 * j + 224, :] = half_silu(acc).astype(jnp.bfloat16)
        stack_layers(ha, hb, we2, C1, 6, 12, 256)
        for l in range(HALF):
            even = ha[64 * l + 32 : 64 * l + 64, :].astype(jnp.float32)
            odd = ha[64 * l + 64 : 64 * l + 96, :].astype(jnp.float32)
            pool[32 * l + 32 : 32 * l + 64, :] = (0.5 * (even + odd)).astype(jnp.bfloat16)
        w = wm1[...]
        for j in range(12):
            acc = dot(w, pool[96 * j : 96 * j + 160, :])
            ma[192 * j + 64 : 192 * j + 256, :] = half_silu(acc).astype(jnp.bfloat16)
        stack_layers(ma, mb, wm2, C2, 2, 18, 256)
        w = wdm[...]
        ws = wds[...]
        for j in range(18):
            acc = dot(w, ma[128 * j : 128 * j + 256, :]) + dot(ws, ha[128 * j : 128 * j + 192, :])
            hc[128 * j + 32 : 128 * j + 160, :] = half_silu(acc).astype(jnp.bfloat16)
        stack_layers(hc, hb, wd2, C1, 6, 12, 256)
        w = wo[...]
        for j in range(12):
            acc = dot(w, hc[192 * j : 192 * j + 256, :])
            for d in range(6):
                for part in range(NB // LANES):
                    wide[part, pl.ds(6 * j + d, F_OUT, stride=LEV), :] = acc[
                        F_OUT * d : F_OUT * (d + 1), part * LANES : (part + 1) * LANES
                    ]
        for part in range(NB // LANES):
            result = wide[part].T
            rows = lax.broadcasted_iota(jnp.int32, result.shape, 0) + part * LANES
            y_ref[part * LANES : (part + 1) * LANES, :] = jnp.where(
                rows < live, result, 0.0
            ).astype(jnp.bfloat16)


def run_net(columns, size, bands):
    rows, feat = columns.shape
    whole = [pl.BlockSpec(b.shape, functools.partial(lambda n, g, s: (0,) * n, b.ndim)) for b in bands]
    lanes = NB
    outer = (LEV + 2) * C1
    inner = (HALF + 2) * C2
    block = pl.BlockSpec((NB, feat), lambda g, s: (g, 0))
    return pl.pallas_call(
        net_kernel,
        out_shape=jax.ShapeDtypeStruct((rows, feat), jnp.bfloat16),
        grid_spec=pltpu.PrefetchScalarGridSpec(
            num_scalar_prefetch=1,
            grid=(rows // NB,),
            in_specs=[block] + whole,
            out_specs=block,
            scratch_shapes=[
                pltpu.VMEM((NB // LANES, FEAT, LANES), jnp.float32),
                pltpu.VMEM(((LEV + 2) * F_IN, lanes), jnp.bfloat16),
                pltpu.VMEM((outer, lanes), jnp.bfloat16),
                pltpu.VMEM((outer, lanes), jnp.bfloat16),
                pltpu.VMEM((outer, lanes), jnp.bfloat16),
                pltpu.VMEM(((HALF + 2) * C1, lanes), jnp.bfloat16),
                pltpu.VMEM((inner, lanes), jnp.bfloat16),
                pltpu.VMEM((inner, lanes), jnp.bfloat16),
            ],
        ),
        compiler_params=pltpu.CompilerParams(vmem_limit_bytes=48 * 1024 * 1024),
    )(size, columns, *bands)


def make_bands(e1, e2, m1, m2, d1, d2, wo):
    half = jnp.bfloat16(0.5)
    return (
        band(e1 * half, 6),
        band(e2 * half, 6),
        band(m1 * half, 3),
        band(m2 * half, 2),
        raised_band(d1[:, :, :C2] * half),
        band(d1[:, :, C2:] * half, 4),
        band(d2 * half, 6),
        band(wo, 6),
    )


def shift(value, axis, step):
    count = lax.axis_size(axis)
    return lax.ppermute(value, axis, [(i, (i + step) % count) for i in range(count)])


def on_device(column_state, counts, edge_index, *weights):
    device_index = lax.axis_index(("elem", "span"))
    bands = make_bands(*weights)
    own = counts[device_index]
    owned = run_net(column_state, own[None], bands)
    edge_local = edge_index[0]
    edge_rows = owned[edge_local]
    from_west = shift(edge_rows[1], "elem", 1)
    from_east = shift(edge_rows[0], "elem", -1)
    from_south = shift(edge_rows[3], "span", 1)
    from_north = shift(edge_rows[2], "span", -1)
    across = jnp.stack([from_west, from_east, from_south, from_north], axis=0)
    merged = 0.5 * (edge_rows.astype(jnp.float32) + across.astype(jnp.float32))
    merged = merged.astype(jnp.bfloat16).reshape(-1, owned.shape[1])
    return owned.at[edge_local.reshape(-1)].set(merged)


def solution(mesh):
    return jax.shard_map(
        on_device,
        mesh=mesh,
        in_specs=(P(("elem", "span"), None), P(), P(("elem", "span"), None, None)) + (P(),) * 7,
        out_specs=P(("elem", "span"), None),
        check_vma=False,
    )
```

```python
import functools

import jax
import jax.numpy as jnp
from jax import lax
from jax.experimental import pallas as pl
from jax.experimental.pallas import tpu as pltpu
from jax.sharding import PartitionSpec as P

LEV = 72
HALF = LEV // 2
F_IN = 16
F_OUT = 16
C1 = 32
C2 = 64
DEPTH = 8
FEAT = F_IN * LEV
LANES = 128
NB = 256


def fill_band(dst, taps, levels, layer=None):
    out, inn = taps[0].shape
    lanes = -(-(levels + 2) * inn // LANES) * LANES
    flat = jnp.concatenate(taps + [jnp.zeros((out, lanes - 3 * inn), jnp.float32)], axis=1)
    for d in range(levels):
        moved = flat if d == 0 else pltpu.roll(flat, d * inn, 1)
        moved = moved[:, : (levels + 2) * inn].astype(jnp.bfloat16)
        if layer is None:
            dst[d * out : (d + 1) * out, :] = moved
        else:
            dst[layer, d * out : (d + 1) * out, :] = moved


def taps_of(ref, scale, layer=None, lo=None, hi=None):
    found = []
    for t in range(3):
        tap = (ref[t] if layer is None else ref[layer, t]).astype(jnp.float32) * scale
        found.append(tap[:, lo:hi])
    return found


def build_bands(raw, bands):
    e1, e2, m1, m2, d1, d2, wo = raw
    be1, be2, bm1, bm2, bdm, bds, bd2, bo = bands
    fill_band(be1, taps_of(e1, 0.5), 6)
    fill_band(bm1, taps_of(m1, 0.5), 3)
    fill_band(bds, taps_of(d1, 0.5, lo=C2, hi=C2 + C1), 4)
    fill_band(bo, taps_of(wo, 1.0), 6)
    w = taps_of(d1, 0.5, lo=0, hi=C2)
    zero = jnp.zeros_like(w[0])
    first, both, late, last = w[0], w[1] + w[2], w[0] + w[1], w[2]
    rows = [
        [first, both, zero, zero],
        [zero, late, last, zero],
        [zero, first, both, zero],
        [zero, zero, late, last],
    ]
    for d, row in enumerate(rows):
        bdm[d * C1 : (d + 1) * C1, :] = jnp.concatenate(row, axis=1).astype(jnp.bfloat16)

    def layer_bands(layer, carry):
        fill_band(be2, taps_of(e2, 0.5, layer), 6, layer)
        fill_band(bm2, taps_of(m2, 0.5, layer), 2, layer)
        fill_band(bd2, taps_of(d2, 0.5, layer), 6, layer)
        return carry

    lax.fori_loop(0, DEPTH, layer_bands, 0)


BAND_SHAPES = (
    (6 * C1, 8 * F_IN),
    (DEPTH, 6 * C1, 8 * C1),
    (3 * C2, 5 * C1),
    (DEPTH, 2 * C2, 4 * C2),
    (4 * C1, 4 * C2),
    (4 * C1, 6 * C1),
    (DEPTH, 6 * C1, 8 * C1),
    (6 * F_OUT, 8 * C1),
)


def half_silu(acc):
    return acc + acc * jnp.tanh(acc)


def dot(a, b):
    return jnp.dot(a, b, preferred_element_type=jnp.float32)


def stack_layers(src, dst, w_ref, channels, per, blocks, width):
    def one(layer, source, target):
        w = w_ref[layer]
        for j in range(blocks):
            lo = j * per * channels
            acc = dot(w, source[lo : lo + width, :])
            mid = slice(lo + channels, lo + channels + per * channels)
            target[mid, :] = source[mid, :] + half_silu(acc).astype(jnp.bfloat16)

    def pair(step, carry):
        one(2 * step, src, dst)
        one(2 * step + 1, dst, src)
        return carry

    lax.fori_loop(0, DEPTH // 2, pair, 0)


def clear(scratch):
    for ref in scratch[1:]:
        ref[...] = jnp.zeros_like(ref)


def block_net(live, x_ref, bands, y_ref, scratch):
    we1, we2, wm1, wm2, wdm, wds, wd2, wo = bands
    wide, xin, ha, hb, hc, pool, ma, mb = scratch
    for part in range(NB // LANES):
        here = slice(part * LANES, (part + 1) * LANES)
        wide[part] = x_ref[here, :].astype(jnp.float32).T
        for l in range(LEV):
            xin[F_IN * (l + 1) : F_IN * (l + 2), here] = wide[
                part, pl.ds(l, F_IN, stride=LEV), :
            ].astype(jnp.bfloat16)
    w = we1[...]
    for j in range(12):
        acc = dot(w, xin[96 * j : 96 * j + 128, :])
        ha[192 * j + 32 : 192 * j + 224, :] = half_silu(acc).astype(jnp.bfloat16)
    stack_layers(ha, hb, we2, C1, 6, 12, 256)
    for l in range(HALF):
        even = ha[64 * l + 32 : 64 * l + 64, :].astype(jnp.float32)
        odd = ha[64 * l + 64 : 64 * l + 96, :].astype(jnp.float32)
        pool[32 * l + 32 : 32 * l + 64, :] = (0.5 * (even + odd)).astype(jnp.bfloat16)
    w = wm1[...]
    for j in range(12):
        acc = dot(w, pool[96 * j : 96 * j + 160, :])
        ma[192 * j + 64 : 192 * j + 256, :] = half_silu(acc).astype(jnp.bfloat16)
    stack_layers(ma, mb, wm2, C2, 2, 18, 256)
    w = wdm[...]
    ws = wds[...]
    for j in range(18):
        acc = dot(w, ma[128 * j : 128 * j + 256, :]) + dot(ws, ha[128 * j : 128 * j + 192, :])
        hc[128 * j + 32 : 128 * j + 160, :] = half_silu(acc).astype(jnp.bfloat16)
    stack_layers(hc, hb, wd2, C1, 6, 12, 256)
    w = wo[...]
    for j in range(12):
        acc = dot(w, hc[192 * j : 192 * j + 256, :])
        for d in range(6):
            for part in range(NB // LANES):
                wide[part, pl.ds(6 * j + d, F_OUT, stride=LEV), :] = acc[
                    F_OUT * d : F_OUT * (d + 1), part * LANES : (part + 1) * LANES
                ]
    for part in range(NB // LANES):
        result = wide[part].T
        rows = lax.broadcasted_iota(jnp.int32, result.shape, 0) + part * LANES
        y_ref[part * LANES : (part + 1) * LANES, :] = jnp.where(
            rows < live, result, 0.0
        ).astype(jnp.bfloat16)


def first_kernel(sizes, x_ref, place, *refs):
    raw, bands, y_ref, edge_ref, scratch = refs[:7], refs[7:15], refs[15], refs[16], refs[17:]
    clear(scratch)
    build_bands(raw, bands)
    block_net(sizes[0], x_ref, bands, y_ref, scratch)
    lanes = lax.broadcasted_iota(jnp.int32, (place.shape[0], NB), 1)
    pick = jnp.where(lanes == place[...], 1.0, 0.0).astype(jnp.bfloat16)
    edge_ref[...] = dot(pick, y_ref[...]).astype(jnp.bfloat16)


def rest_kernel(sizes, x_ref, last_ref, *refs):
    bands, y_ref, scratch = refs[:8], refs[8], refs[9:]
    step = pl.program_id(0)
    live = sizes[step]

    @pl.when(step == 0)
    def _():
        clear(scratch)

    @pl.when(live <= 0)
    def _():
        y_ref[...] = jnp.zeros_like(y_ref)

    @pl.when(jnp.logical_and(live > 0, step == 0))
    def _():
        scratch[8][...] = x_ref[...]

    @pl.when(jnp.logical_and(live > 0, step > 0))
    def _():
        scratch[8][...] = last_ref[...]

    @pl.when(live > 0)
    def _():
        block_net(live, scratch[8], bands, y_ref, scratch[:8])


def final_kernel(sizes, y0, rest, back, place, edges, west, east, south, north, out):
    count, moved, offset = sizes[0], sizes[1], sizes[2]
    across = jnp.concatenate([r[...].astype(jnp.float32) for r in (west, east, south, north)], axis=0)
    merged = (0.5 * (edges[...].astype(jnp.float32) + across)).astype(jnp.bfloat16)
    rows = lax.broadcasted_iota(jnp.int32, (NB, merged.shape[0]), 0)
    pick = jnp.where(rows == place[...], 1.0, 0.0)
    hit = jnp.sum(pick, axis=1, keepdims=True) > 0.0
    chosen = dot(pick.astype(jnp.bfloat16), merged)
    out[0:NB, :] = jnp.where(hit, chosen, y0[...].astype(jnp.float32)).astype(jnp.bfloat16)
    at = lax.broadcasted_iota(jnp.int32, (NB, 1), 0)
    out[NB : 2 * NB, :] = jnp.where(
        at + NB < count, rest[0:NB, :].astype(jnp.float32), 0.0
    ).astype(jnp.bfloat16)

    @pl.when(moved == 0)
    def _():
        out[2 * NB : 3 * NB, :] = rest[NB : 2 * NB, :]

    @pl.when(moved > 0)
    def _():
        turned = pltpu.roll(back[...].astype(jnp.float32), lax.rem(NB - offset, NB), 0)
        out[2 * NB : 3 * NB, :] = jnp.where(at + 2 * NB < count, turned, 0.0).astype(jnp.bfloat16)


def whole_spec(shape):
    return pl.BlockSpec(shape, lambda *_: (0,) * len(shape))


def net_scratch():
    outer = (LEV + 2) * C1
    inner = (HALF + 2) * C2
    return [
        pltpu.VMEM((NB // LANES, FEAT, LANES), jnp.float32),
        pltpu.VMEM(((LEV + 2) * F_IN, NB), jnp.bfloat16),
        pltpu.VMEM((outer, NB), jnp.bfloat16),
        pltpu.VMEM((outer, NB), jnp.bfloat16),
        pltpu.VMEM((outer, NB), jnp.bfloat16),
        pltpu.VMEM(((HALF + 2) * C1, NB), jnp.bfloat16),
        pltpu.VMEM((inner, NB), jnp.bfloat16),
        pltpu.VMEM((inner, NB), jnp.bfloat16),
    ]


def bf16(*shape):
    return jax.ShapeDtypeStruct(shape, jnp.bfloat16)


def call(kernel, out_shape, grid, in_specs, out_specs, scratch, flops, operands):
    return pl.pallas_call(
        kernel,
        out_shape=out_shape,
        grid_spec=pltpu.PrefetchScalarGridSpec(
            num_scalar_prefetch=1,
            grid=grid,
            in_specs=in_specs,
            out_specs=out_specs,
            scratch_shapes=scratch,
        ),
        compiler_params=pltpu.CompilerParams(vmem_limit_bytes=48 * 1024 * 1024),
        cost_estimate=pl.CostEstimate(flops=flops, bytes_accessed=4000000, transcendentals=0),
    )(*operands)


def run_first(columns, size, place, weights):
    entries = place.shape[0]
    block = whole_spec((NB, FEAT))
    shapes = BAND_SHAPES + ((NB, FEAT), (entries, FEAT))
    found = call(
        first_kernel,
        [bf16(*shape) for shape in shapes],
        (1,),
        [block, whole_spec(place.shape)] + [whole_spec(w.shape) for w in weights],
        [whole_spec(shape) for shape in shapes],
        net_scratch(),
        15 * 10**9,
        (size, columns, place) + tuple(weights),
    )
    return found[:8], found[8], found[9]


def run_rest(second, columns, sizes, bands):
    block = pl.BlockSpec((NB, FEAT), lambda g, s: (0, 0))
    last = pl.BlockSpec((NB, FEAT), lambda g, s: (2, 0))
    return call(
        rest_kernel,
        bf16(2 * NB, FEAT),
        (2,),
        [block, last] + [whole_spec(b.shape) for b in bands],
        pl.BlockSpec((NB, FEAT), lambda g, s: (g, 0)),
        net_scratch() + [pltpu.VMEM((NB, FEAT), jnp.bfloat16)],
        20 * 10**9,
        (sizes, second, columns) + tuple(bands),
    )


def run_final(sizes, operands, rows):
    return call(
        final_kernel,
        bf16(rows, FEAT),
        (1,),
        [whole_spec(v.shape) for v in operands],
        whole_spec((rows, FEAT)),
        [],
        10**8,
        (sizes,) + tuple(operands),
    )


def shift(value, axis, step):
    count = lax.axis_size(axis)
    return lax.ppermute(value, axis, [(i, (i + step) % count) for i in range(count)])


def on_device(column_state, counts, edge_index, *weights):
    device_index = lax.axis_index(("elem", "span"))
    span = lax.axis_size("span")
    own = counts[device_index]
    other = counts[device_index ^ 1]
    fits = own + other <= 4 * NB
    gives = jnp.logical_and(fits, own > 2 * NB)
    takes = jnp.logical_and(fits, other > 2 * NB)
    offset_out = jnp.maximum(other, NB) - NB
    offset_in = jnp.maximum(own, NB) - NB
    swap = [(i, i ^ 1) for i in range(span)]

    start = jnp.clip(2 * NB - offset_out, 0, column_state.shape[0] - NB)
    slab = lax.dynamic_slice_in_dim(column_state, start, NB, axis=0)
    arrived = lax.ppermute(slab, "span", swap)

    edge_flat = edge_index.reshape(-1)
    bands, y0, edge_rows = run_first(column_state, own[None], edge_flat[:, None], weights)
    side = edge_rows.reshape(4, -1, FEAT)
    from_west = shift(side[1], "elem", 1)
    from_east = shift(side[0], "elem", -1)
    from_south = shift(side[3], "span", 1)
    from_north = shift(side[2], "span", -1)

    at = jnp.arange(NB, dtype=jnp.int32)[:, None]
    second = jnp.where(
        jnp.logical_and(takes, at >= offset_in), arrived, column_state[NB : 2 * NB]
    )
    live_second = jnp.where(takes, offset_in + other - 2 * NB, jnp.minimum(own - NB, NB))
    live_last = jnp.where(gives, 0, own - 2 * NB)
    rest = run_rest(second, column_state, jnp.stack([live_second, live_last]), bands)
    back = lax.ppermute(rest[:NB], "span", swap)
    sizes = jnp.stack([own, gives.astype(jnp.int32), jnp.clip(offset_out, 0, NB)])
    return run_final(
        sizes,
        (y0, rest, back, edge_flat[None, :], edge_rows, from_west, from_east, from_south, from_north),
        column_state.shape[0],
    )


def solution(mesh):
    return jax.shard_map(
        on_device,
        mesh=mesh,
        in_specs=(P(("elem", "span"), None), P(), P(("elem", "span"), None, None)) + (P(),) * 7,
        out_specs=P(("elem", "span"), None),
        check_vma=False,
    )
```

```python
import functools

import jax
import jax.numpy as jnp
from jax import lax
from jax.experimental import pallas as pl
from jax.experimental.pallas import tpu as pltpu
from jax.sharding import PartitionSpec as P

LEV = 72
HALF = LEV // 2
F_IN = 16
F_OUT = 16
C1 = 32
C2 = 64
DEPTH = 8
FEAT = F_IN * LEV
LANES = 128
NB = 256


def fill_band(dst, taps, levels, layer=None):
    out, inn = taps[0].shape
    lanes = -(-(levels + 2) * inn // LANES) * LANES
    flat = jnp.concatenate(taps + [jnp.zeros((out, lanes - 3 * inn), jnp.float32)], axis=1)
    for d in range(levels):
        moved = flat if d == 0 else pltpu.roll(flat, d * inn, 1)
        moved = moved[:, : (levels + 2) * inn].astype(jnp.bfloat16)
        if layer is None:
            dst[d * out : (d + 1) * out, :] = moved
        else:
            dst[layer, d * out : (d + 1) * out, :] = moved


def taps_of(ref, scale, layer=None, lo=None, hi=None):
    found = []
    for t in range(3):
        tap = (ref[t] if layer is None else ref[layer, t]).astype(jnp.float32) * scale
        found.append(tap[:, lo:hi])
    return found


def build_bands(raw, bands):
    e1, e2, m1, m2, d1, d2, wo = raw
    be1, be2, bm1, bm2, bdm, bds, bd2, bo = bands
    fill_band(be1, taps_of(e1, 0.5), 6)
    fill_band(bm1, taps_of(m1, 0.5), 3)
    fill_band(bds, taps_of(d1, 0.5, lo=C2, hi=C2 + C1), 4)
    fill_band(bo, taps_of(wo, 1.0), 6)
    w = taps_of(d1, 0.5, lo=0, hi=C2)
    zero = jnp.zeros_like(w[0])
    first, both, late, last = w[0], w[1] + w[2], w[0] + w[1], w[2]
    rows = [
        [first, both, zero, zero],
        [zero, late, last, zero],
        [zero, first, both, zero],
        [zero, zero, late, last],
    ]
    for d, row in enumerate(rows):
        bdm[d * C1 : (d + 1) * C1, :] = jnp.concatenate(row, axis=1).astype(jnp.bfloat16)

    def layer_bands(layer, carry):
        fill_band(be2, taps_of(e2, 0.5, layer), 6, layer)
        fill_band(bm2, taps_of(m2, 0.5, layer), 2, layer)
        fill_band(bd2, taps_of(d2, 0.5, layer), 6, layer)
        return carry

    lax.fori_loop(0, DEPTH, layer_bands, 0)


BAND_SHAPES = (
    (6 * C1, 8 * F_IN),
    (DEPTH, 6 * C1, 8 * C1),
    (3 * C2, 5 * C1),
    (DEPTH, 2 * C2, 4 * C2),
    (4 * C1, 4 * C2),
    (4 * C1, 6 * C1),
    (DEPTH, 6 * C1, 8 * C1),
    (6 * F_OUT, 8 * C1),
)


def half_silu(acc):
    return acc + acc * jnp.tanh(acc)


def dot(a, b):
    return jnp.dot(a, b, preferred_element_type=jnp.float32)


def stack_layers(src, dst, w_ref, channels, per, blocks, width):
    def one(layer, source, target):
        w = w_ref[layer]
        for j in range(blocks):
            lo = j * per * channels
            acc = dot(w, source[lo : lo + width, :])
            mid = slice(lo + channels, lo + channels + per * channels)
            target[mid, :] = source[mid, :] + half_silu(acc).astype(jnp.bfloat16)

    def pair(step, carry):
        one(2 * step, src, dst)
        one(2 * step + 1, dst, src)
        return carry

    lax.fori_loop(0, DEPTH // 2, pair, 0)


def clear(scratch):
    for ref in scratch[1:]:
        ref[...] = jnp.zeros_like(ref)


def block_net(live, x_ref, bands, y_ref, scratch):
    we1, we2, wm1, wm2, wdm, wds, wd2, wo = bands
    wide, xin, ha, hb, hc, pool, ma, mb = scratch
    for part in range(NB // LANES):
        here = slice(part * LANES, (part + 1) * LANES)
        wide[part] = x_ref[here, :].astype(jnp.float32).T
        for l in range(LEV):
            xin[F_IN * (l + 1) : F_IN * (l + 2), here] = wide[
                part, pl.ds(l, F_IN, stride=LEV), :
            ].astype(jnp.bfloat16)
    w = we1[...]
    for j in range(12):
        acc = dot(w, xin[96 * j : 96 * j + 128, :])
        ha[192 * j + 32 : 192 * j + 224, :] = half_silu(acc).astype(jnp.bfloat16)
    stack_layers(ha, hb, we2, C1, 6, 12, 256)
    for l in range(HALF):
        even = ha[64 * l + 32 : 64 * l + 64, :].astype(jnp.float32)
        odd = ha[64 * l + 64 : 64 * l + 96, :].astype(jnp.float32)
        pool[32 * l + 32 : 32 * l + 64, :] = (0.5 * (even + odd)).astype(jnp.bfloat16)
    w = wm1[...]
    for j in range(12):
        acc = dot(w, pool[96 * j : 96 * j + 160, :])
        ma[192 * j + 64 : 192 * j + 256, :] = half_silu(acc).astype(jnp.bfloat16)
    stack_layers(ma, mb, wm2, C2, 2, 18, 256)
    w = wdm[...]
    ws = wds[...]
    for j in range(18):
        acc = dot(w, ma[128 * j : 128 * j + 256, :]) + dot(ws, ha[128 * j : 128 * j + 192, :])
        hc[128 * j + 32 : 128 * j + 160, :] = half_silu(acc).astype(jnp.bfloat16)
    stack_layers(hc, hb, wd2, C1, 6, 12, 256)
    w = wo[...]
    for j in range(12):
        acc = dot(w, hc[192 * j : 192 * j + 256, :])
        for d in range(6):
            for part in range(NB // LANES):
                wide[part, pl.ds(6 * j + d, F_OUT, stride=LEV), :] = acc[
                    F_OUT * d : F_OUT * (d + 1), part * LANES : (part + 1) * LANES
                ]
    for part in range(NB // LANES):
        result = wide[part].T
        rows = lax.broadcasted_iota(jnp.int32, result.shape, 0) + part * LANES
        y_ref[part * LANES : (part + 1) * LANES, :] = jnp.where(
            rows < live, result, 0.0
        ).astype(jnp.bfloat16)


def first_kernel(sizes, x_ref, place, *refs):
    raw, y_ref, edge_ref, bands, scratch = refs[:7], refs[7], refs[8], refs[9:17], refs[17:]
    clear(scratch)
    build_bands(raw, bands)
    block_net(sizes[0], x_ref, bands, y_ref, scratch)
    lanes = lax.broadcasted_iota(jnp.int32, (place.shape[0], NB), 1)
    pick = jnp.where(lanes == place[...], 1.0, 0.0).astype(jnp.bfloat16)
    edge_ref[...] = dot(pick, y_ref[...]).astype(jnp.bfloat16)


def rest_kernel(sizes, x_ref, last_ref, *refs):
    raw, y_ref, bands, scratch = refs[:7], refs[7], refs[8:16], refs[16:]
    step = pl.program_id(0)
    live = sizes[step]

    @pl.when(jnp.logical_and(step == 0, jnp.maximum(live, sizes[1]) > 0))
    def _():
        clear(scratch[:8])
        build_bands(raw, bands)

    @pl.when(live <= 0)
    def _():
        y_ref[...] = jnp.zeros_like(y_ref)

    @pl.when(jnp.logical_and(live > 0, step == 0))
    def _():
        scratch[8][...] = x_ref[...]

    @pl.when(jnp.logical_and(live > 0, step > 0))
    def _():
        scratch[8][...] = last_ref[...]

    @pl.when(live > 0)
    def _():
        block_net(live, scratch[8], bands, y_ref, scratch[:8])


def final_kernel(sizes, y0, rest, back, place, edges, west, east, south, north, out):
    count, moved, offset = sizes[0], sizes[1], sizes[2]
    across = jnp.concatenate([r[...].astype(jnp.float32) for r in (west, east, south, north)], axis=0)
    merged = (0.5 * (edges[...].astype(jnp.float32) + across)).astype(jnp.bfloat16)
    rows = lax.broadcasted_iota(jnp.int32, (NB, merged.shape[0]), 0)
    pick = jnp.where(rows == place[...], 1.0, 0.0)
    hit = jnp.sum(pick, axis=1, keepdims=True) > 0.0
    chosen = dot(pick.astype(jnp.bfloat16), merged)
    out[0:NB, :] = jnp.where(hit, chosen, y0[...].astype(jnp.float32)).astype(jnp.bfloat16)
    at = lax.broadcasted_iota(jnp.int32, (NB, 1), 0)
    out[NB : 2 * NB, :] = jnp.where(
        at + NB < count, rest[0:NB, :].astype(jnp.float32), 0.0
    ).astype(jnp.bfloat16)

    @pl.when(moved == 0)
    def _():
        out[2 * NB : 3 * NB, :] = rest[NB : 2 * NB, :]

    @pl.when(moved > 0)
    def _():
        turned = pltpu.roll(back[...].astype(jnp.float32), lax.rem(NB - offset, NB), 0)
        out[2 * NB : 3 * NB, :] = jnp.where(at + 2 * NB < count, turned, 0.0).astype(jnp.bfloat16)


def whole_spec(shape):
    return pl.BlockSpec(shape, lambda *_: (0,) * len(shape))


def net_scratch():
    outer = (LEV + 2) * C1
    inner = (HALF + 2) * C2
    return [pltpu.VMEM(shape, jnp.bfloat16) for shape in BAND_SHAPES] + [
        pltpu.VMEM((NB // LANES, FEAT, LANES), jnp.float32),
        pltpu.VMEM(((LEV + 2) * F_IN, NB), jnp.bfloat16),
        pltpu.VMEM((outer, NB), jnp.bfloat16),
        pltpu.VMEM((outer, NB), jnp.bfloat16),
        pltpu.VMEM((outer, NB), jnp.bfloat16),
        pltpu.VMEM(((HALF + 2) * C1, NB), jnp.bfloat16),
        pltpu.VMEM((inner, NB), jnp.bfloat16),
        pltpu.VMEM((inner, NB), jnp.bfloat16),
    ]


def bf16(*shape):
    return jax.ShapeDtypeStruct(shape, jnp.bfloat16)


def call(kernel, out_shape, grid, in_specs, out_specs, scratch, flops, operands):
    return pl.pallas_call(
        kernel,
        out_shape=out_shape,
        grid_spec=pltpu.PrefetchScalarGridSpec(
            num_scalar_prefetch=1,
            grid=grid,
            in_specs=in_specs,
            out_specs=out_specs,
            scratch_shapes=scratch,
        ),
        cost_estimate=pl.CostEstimate(flops=flops, bytes_accessed=4000000, transcendentals=0),
    )(*operands)


def run_first(columns, size, place, weights):
    entries = place.shape[0]
    block = whole_spec((NB, FEAT))
    shapes = ((NB, FEAT), (entries, FEAT))
    return call(
        first_kernel,
        [bf16(*shape) for shape in shapes],
        (1,),
        [block, whole_spec(place.shape)] + [whole_spec(w.shape) for w in weights],
        [whole_spec(shape) for shape in shapes],
        net_scratch(),
        15 * 10**9,
        (size, columns, place) + tuple(weights),
    )


def run_rest(second, columns, sizes, weights):
    block = pl.BlockSpec((NB, FEAT), lambda g, s: (0, 0))
    last = pl.BlockSpec((NB, FEAT), lambda g, s: (2, 0))
    return call(
        rest_kernel,
        bf16(2 * NB, FEAT),
        (2,),
        [block, last] + [whole_spec(w.shape) for w in weights],
        pl.BlockSpec((NB, FEAT), lambda g, s: (g, 0)),
        net_scratch() + [pltpu.VMEM((NB, FEAT), jnp.bfloat16)],
        20 * 10**9,
        (sizes, second, columns) + tuple(weights),
    )


def run_final(sizes, operands, rows):
    return call(
        final_kernel,
        bf16(rows, FEAT),
        (1,),
        [whole_spec(v.shape) for v in operands],
        whole_spec((rows, FEAT)),
        [],
        10**8,
        (sizes,) + tuple(operands),
    )


def shift(value, axis, step):
    count = lax.axis_size(axis)
    return lax.ppermute(value, axis, [(i, (i + step) % count) for i in range(count)])


def on_device(column_state, counts, edge_index, *weights):
    device_index = lax.axis_index(("elem", "span"))
    span = lax.axis_size("span")
    own = counts[device_index]
    other = counts[device_index ^ 1]
    fits = own + other <= 4 * NB
    gives = jnp.logical_and(fits, own > 2 * NB)
    takes = jnp.logical_and(fits, other > 2 * NB)
    offset_out = jnp.maximum(other, NB) - NB
    offset_in = jnp.maximum(own, NB) - NB
    swap = [(i, i ^ 1) for i in range(span)]

    start = jnp.clip(2 * NB - offset_out, 0, column_state.shape[0] - NB)
    slab = lax.dynamic_slice_in_dim(column_state, start, NB, axis=0)
    arrived = lax.ppermute(slab, "span", swap)

    edge_flat = edge_index.reshape(-1)
    y0, edge_rows = run_first(column_state, own[None], edge_flat[:, None], weights)
    side = edge_rows.reshape(4, -1, FEAT)
    from_west = shift(side[1], "elem", 1)
    from_east = shift(side[0], "elem", -1)
    from_south = shift(side[3], "span", 1)
    from_north = shift(side[2], "span", -1)

    at = jnp.arange(NB, dtype=jnp.int32)[:, None]
    second = jnp.where(
        jnp.logical_and(takes, at >= offset_in), arrived, column_state[NB : 2 * NB]
    )
    live_second = jnp.where(takes, offset_in + other - 2 * NB, jnp.minimum(own - NB, NB))
    live_last = jnp.where(gives, 0, own - 2 * NB)
    rest = run_rest(second, column_state, jnp.stack([live_second, live_last]), weights)
    back = lax.ppermute(rest[:NB], "span", swap)
    sizes = jnp.stack([own, gives.astype(jnp.int32), jnp.clip(offset_out, 0, NB)])
    return run_final(
        sizes,
        (y0, rest, back, edge_flat[None, :], edge_rows, from_west, from_east, from_south, from_north),
        column_state.shape[0],
    )


def solution(mesh):
    return jax.shard_map(
        on_device,
        mesh=mesh,
        in_specs=(P(("elem", "span"), None), P(), P(("elem", "span"), None, None)) + (P(),) * 7,
        out_specs=P(("elem", "span"), None),
        check_vma=False,
    )
```

```python
import functools

import jax
import jax.numpy as jnp
from jax import lax
from jax.experimental import pallas as pl
from jax.experimental.pallas import tpu as pltpu
from jax.sharding import PartitionSpec as P

LEV = 72
HALF = LEV // 2
F_IN = 16
F_OUT = 16
C1 = 32
C2 = 64
DEPTH = 8
FEAT = F_IN * LEV
LANES = 128
NB = 256


def fill_band(dst, taps, levels, layer=None):
    out, inn = taps[0].shape
    lanes = -(-(levels + 2) * inn // LANES) * LANES
    flat = jnp.concatenate(taps + [jnp.zeros((out, lanes - 3 * inn), jnp.float32)], axis=1)
    for d in range(levels):
        moved = flat if d == 0 else pltpu.roll(flat, d * inn, 1)
        moved = moved[:, : (levels + 2) * inn].astype(jnp.bfloat16)
        if layer is None:
            dst[d * out : (d + 1) * out, :] = moved
        else:
            dst[layer, d * out : (d + 1) * out, :] = moved


def taps_of(ref, scale, layer=None, lo=None, hi=None):
    found = []
    for t in range(3):
        tap = (ref[t] if layer is None else ref[layer, t]).astype(jnp.float32) * scale
        found.append(tap[:, lo:hi])
    return found


def build_bands(raw, bands):
    e1, e2, m1, m2, d1, d2, wo = raw
    be1, be2, bm1, bm2, bdm, bds, bd2, bo = bands
    fill_band(be1, taps_of(e1, 0.5), 6)
    fill_band(bm1, taps_of(m1, 0.5), 3)
    fill_band(bds, taps_of(d1, 0.5, lo=C2, hi=C2 + C1), 4)
    fill_band(bo, taps_of(wo, 1.0), 6)
    w = taps_of(d1, 0.5, lo=0, hi=C2)
    zero = jnp.zeros_like(w[0])
    first, both, late, last = w[0], w[1] + w[2], w[0] + w[1], w[2]
    rows = [
        [first, both, zero, zero],
        [zero, late, last, zero],
        [zero, first, both, zero],
        [zero, zero, late, last],
    ]
    for d, row in enumerate(rows):
        bdm[d * C1 : (d + 1) * C1, :] = jnp.concatenate(row, axis=1).astype(jnp.bfloat16)

    def layer_bands(layer, carry):
        fill_band(be2, taps_of(e2, 0.5, layer), 6, layer)
        fill_band(bm2, taps_of(m2, 0.5, layer), 2, layer)
        fill_band(bd2, taps_of(d2, 0.5, layer), 6, layer)
        return carry

    lax.fori_loop(0, DEPTH, layer_bands, 0)


BAND_SHAPES = (
    (6 * C1, 8 * F_IN),
    (DEPTH, 6 * C1, 8 * C1),
    (3 * C2, 5 * C1),
    (DEPTH, 2 * C2, 4 * C2),
    (4 * C1, 4 * C2),
    (4 * C1, 6 * C1),
    (DEPTH, 6 * C1, 8 * C1),
    (6 * F_OUT, 8 * C1),
)


def half_silu(acc):
    return acc + acc * jnp.tanh(acc)


def dot(a, b):
    return jnp.dot(a, b, preferred_element_type=jnp.float32)


def stack_layers(src, dst, w_ref, channels, per, blocks, width):
    def one(layer, source, target):
        w = w_ref[layer]
        for j in range(blocks):
            lo = j * per * channels
            acc = dot(w, source[lo : lo + width, :])
            mid = slice(lo + channels, lo + channels + per * channels)
            target[mid, :] = source[mid, :] + half_silu(acc).astype(jnp.bfloat16)

    def pair(step, carry):
        one(2 * step, src, dst)
        one(2 * step + 1, dst, src)
        return carry

    lax.fori_loop(0, DEPTH // 2, pair, 0)


def clear(scratch):
    for ref in scratch[1:]:
        ref[...] = jnp.zeros_like(ref)


def block_net(live, x_ref, bands, y_ref, scratch):
    we1, we2, wm1, wm2, wdm, wds, wd2, wo = bands
    wide, xin, ha, hb, hc, pool, ma, mb = scratch
    for part in range(NB // LANES):
        here = slice(part * LANES, (part + 1) * LANES)
        wide[part] = x_ref[here, :].astype(jnp.float32).T
        for l in range(LEV):
            xin[F_IN * (l + 1) : F_IN * (l + 2), here] = wide[
                part, pl.ds(l, F_IN, stride=LEV), :
            ].astype(jnp.bfloat16)
    w = we1[...]
    for j in range(12):
        acc = dot(w, xin[96 * j : 96 * j + 128, :])
        ha[192 * j + 32 : 192 * j + 224, :] = half_silu(acc).astype(jnp.bfloat16)
    stack_layers(ha, hb, we2, C1, 6, 12, 256)
    for l in range(HALF):
        even = ha[64 * l + 32 : 64 * l + 64, :].astype(jnp.float32)
        odd = ha[64 * l + 64 : 64 * l + 96, :].astype(jnp.float32)
        pool[32 * l + 32 : 32 * l + 64, :] = (0.5 * (even + odd)).astype(jnp.bfloat16)
    w = wm1[...]
    for j in range(12):
        acc = dot(w, pool[96 * j : 96 * j + 160, :])
        ma[192 * j + 64 : 192 * j + 256, :] = half_silu(acc).astype(jnp.bfloat16)
    stack_layers(ma, mb, wm2, C2, 2, 18, 256)
    w = wdm[...]
    ws = wds[...]
    for j in range(18):
        acc = dot(w, ma[128 * j : 128 * j + 256, :]) + dot(ws, ha[128 * j : 128 * j + 192, :])
        hc[128 * j + 32 : 128 * j + 160, :] = half_silu(acc).astype(jnp.bfloat16)
    stack_layers(hc, hb, wd2, C1, 6, 12, 256)
    w = wo[...]
    for j in range(12):
        acc = dot(w, hc[192 * j : 192 * j + 256, :])
        for d in range(6):
            for part in range(NB // LANES):
                wide[part, pl.ds(6 * j + d, F_OUT, stride=LEV), :] = acc[
                    F_OUT * d : F_OUT * (d + 1), part * LANES : (part + 1) * LANES
                ]
    for part in range(NB // LANES):
        result = wide[part].T
        rows = lax.broadcasted_iota(jnp.int32, result.shape, 0) + part * LANES
        y_ref[part * LANES : (part + 1) * LANES, :] = jnp.where(
            rows < live, result, 0.0
        ).astype(jnp.bfloat16)


def first_kernel(sizes, x_ref, place, *refs):
    raw, y_ref, edge_ref, bands, scratch = refs[:7], refs[7], refs[8], refs[9:17], refs[17:]
    clear(scratch)
    build_bands(raw, bands)
    block_net(sizes[0], x_ref, bands, y_ref, scratch)
    lanes = lax.broadcasted_iota(jnp.int32, (place.shape[0], NB), 1)
    pick = jnp.where(lanes == place[...], 1.0, 0.0).astype(jnp.bfloat16)
    edge_ref[...] = dot(pick, y_ref[...]).astype(jnp.bfloat16)


def rest_kernel(sizes, x_ref, last_ref, *refs):
    raw, y_ref, bands, scratch = refs[:7], refs[7], refs[8:16], refs[16:]
    step = pl.program_id(0)
    live = sizes[step]

    @pl.when(jnp.logical_and(step == 0, jnp.maximum(live, sizes[1]) > 0))
    def _():
        clear(scratch[:8])
        build_bands(raw, bands)

    @pl.when(live <= 0)
    def _():
        y_ref[...] = jnp.zeros_like(y_ref)

    @pl.when(jnp.logical_and(live > 0, step == 0))
    def _():
        scratch[8][...] = x_ref[...]

    @pl.when(jnp.logical_and(live > 0, step > 0))
    def _():
        scratch[8][...] = last_ref[...]

    @pl.when(live > 0)
    def _():
        block_net(live, scratch[8], bands, y_ref, scratch[:8])


def final_kernel(sizes, y0, rest, back, place, edges, west, east, south, north, out):
    count, moved, offset = sizes[0], sizes[1], sizes[2]
    across = jnp.concatenate([r[...].astype(jnp.float32) for r in (west, east, south, north)], axis=0)
    merged = (0.5 * (edges[...].astype(jnp.float32) + across)).astype(jnp.bfloat16)
    rows = lax.broadcasted_iota(jnp.int32, (NB, merged.shape[0]), 0)
    pick = jnp.where(rows == place[...], 1.0, 0.0)
    hit = jnp.sum(pick, axis=1, keepdims=True) > 0.0
    chosen = dot(pick.astype(jnp.bfloat16), merged)
    out[0:NB, :] = jnp.where(hit, chosen, y0[...].astype(jnp.float32)).astype(jnp.bfloat16)
    at = lax.broadcasted_iota(jnp.int32, (NB, 1), 0)
    out[NB : 2 * NB, :] = jnp.where(
        at + NB < count, rest[0:NB, :].astype(jnp.float32), 0.0
    ).astype(jnp.bfloat16)

    @pl.when(moved == 0)
    def _():
        out[2 * NB : 3 * NB, :] = rest[NB : 2 * NB, :]

    @pl.when(moved > 0)
    def _():
        turned = pltpu.roll(back[...].astype(jnp.float32), lax.rem(NB - offset, NB), 0)
        out[2 * NB : 3 * NB, :] = jnp.where(at + 2 * NB < count, turned, 0.0).astype(jnp.bfloat16)


def whole_spec(shape):
    return pl.BlockSpec(shape, lambda *_: (0,) * len(shape))


def net_scratch():
    outer = (LEV + 2) * C1
    inner = (HALF + 2) * C2
    return [pltpu.VMEM(shape, jnp.bfloat16) for shape in BAND_SHAPES] + [
        pltpu.VMEM((NB // LANES, FEAT, LANES), jnp.float32),
        pltpu.VMEM(((LEV + 2) * F_IN, NB), jnp.bfloat16),
        pltpu.VMEM((outer, NB), jnp.bfloat16),
        pltpu.VMEM((outer, NB), jnp.bfloat16),
        pltpu.VMEM((outer, NB), jnp.bfloat16),
        pltpu.VMEM(((HALF + 2) * C1, NB), jnp.bfloat16),
        pltpu.VMEM((inner, NB), jnp.bfloat16),
        pltpu.VMEM((inner, NB), jnp.bfloat16),
    ]


def bf16(*shape):
    return jax.ShapeDtypeStruct(shape, jnp.bfloat16)


def call(kernel, out_shape, grid, in_specs, out_specs, scratch, flops, operands):
    return pl.pallas_call(
        kernel,
        out_shape=out_shape,
        grid_spec=pltpu.PrefetchScalarGridSpec(
            num_scalar_prefetch=1,
            grid=grid,
            in_specs=in_specs,
            out_specs=out_specs,
            scratch_shapes=scratch,
        ),
        cost_estimate=pl.CostEstimate(flops=flops, bytes_accessed=4000000, transcendentals=0),
    )(*operands)


def run_first(columns, size, place, weights):
    entries = place.shape[0]
    block = whole_spec((NB, FEAT))
    shapes = ((NB, FEAT), (entries, FEAT))
    return call(
        first_kernel,
        [bf16(*shape) for shape in shapes],
        (1,),
        [block, whole_spec(place.shape)] + [whole_spec(w.shape) for w in weights],
        [whole_spec(shape) for shape in shapes],
        net_scratch(),
        15 * 10**9,
        (size, columns, place) + tuple(weights),
    )


def run_rest(second, columns, sizes, weights):
    block = pl.BlockSpec((NB, FEAT), lambda g, s: (0, 0))
    last = pl.BlockSpec((NB, FEAT), lambda g, s: (2, 0))
    return call(
        rest_kernel,
        bf16(2 * NB, FEAT),
        (2,),
        [block, last] + [whole_spec(w.shape) for w in weights],
        pl.BlockSpec((NB, FEAT), lambda g, s: (g, 0)),
        net_scratch() + [pltpu.VMEM((NB, FEAT), jnp.bfloat16)],
        20 * 10**9,
        (sizes, second, columns) + tuple(weights),
    )


def run_final(sizes, operands, rows):
    return call(
        final_kernel,
        bf16(rows, FEAT),
        (1,),
        [whole_spec(v.shape) for v in operands],
        whole_spec((rows, FEAT)),
        [],
        10**8,
        (sizes,) + tuple(operands),
    )


def shift(value, axis, step):
    count = lax.axis_size(axis)
    return lax.ppermute(value, axis, [(i, (i + step) % count) for i in range(count)])


def on_device(column_state, counts, edge_index, *weights):
    device_index = lax.axis_index(("elem", "span"))
    span = lax.axis_size("span")
    own = counts[device_index]
    other = counts[device_index ^ 1]
    fits = own + other <= 4 * NB
    gives = jnp.logical_and(fits, own > 2 * NB)
    takes = jnp.logical_and(fits, other > 2 * NB)
    offset_out = jnp.maximum(other, NB) - NB
    offset_in = jnp.maximum(own, NB) - NB
    swap = [(i, i ^ 1) for i in range(span)]

    start = jnp.clip(2 * NB - offset_out, 0, column_state.shape[0] - NB)
    slab = lax.dynamic_slice_in_dim(column_state, start, NB, axis=0)
    arrived = lax.ppermute(slab, "span", swap)

    edge_flat = edge_index.reshape(-1)
    y0, edge_rows = run_first(column_state, own[None], edge_flat[:, None], weights)
    side = edge_rows.reshape(4, -1, FEAT)
    from_west = shift(side[1], "elem", 1)
    from_east = shift(side[0], "elem", -1)
    from_south = shift(side[3], "span", 1)
    from_north = shift(side[2], "span", -1)

    arrived, y0 = lax.optimization_barrier((arrived, y0))
    at = jnp.arange(NB, dtype=jnp.int32)[:, None]
    second = jnp.where(
        jnp.logical_and(takes, at >= offset_in), arrived, column_state[NB : 2 * NB]
    )
    live_second = jnp.where(takes, offset_in + other - 2 * NB, jnp.minimum(own - NB, NB))
    live_last = jnp.where(gives, 0, own - 2 * NB)
    rest = run_rest(second, column_state, jnp.stack([live_second, live_last]), weights)
    back = lax.ppermute(rest[:NB], "span", swap)
    sizes = jnp.stack([own, gives.astype(jnp.int32), jnp.clip(offset_out, 0, NB)])
    return run_final(
        sizes,
        (y0, rest, back, edge_flat[None, :], edge_rows, from_west, from_east, from_south, from_north),
        column_state.shape[0],
    )


def solution(mesh):
    return jax.shard_map(
        on_device,
        mesh=mesh,
        in_specs=(P(("elem", "span"), None), P(), P(("elem", "span"), None, None)) + (P(),) * 7,
        out_specs=P(("elem", "span"), None),
        check_vma=False,
    )
```
